32 devices in a mesh: bel: 8 (over z, x), st: 4 (over y, core).
Axes of the slice: x: 2, y: 2, z: 4, core: 2. Of those that a mesh axis runs over, the one named last changes fastest.
Arguments:
- alphas: bfloat16 [512, 12288], P(None, 'st'), may hold values from -120 to 120
- transitions: bfloat16 [6, 12288, 12288], P(None, 'bel', 'st'), may hold values from 0.0009994507 to 10
- observe: bfloat16 [6, 48, 12288], P(None, None, 'st'), may hold values from 0.0019989014 to 0.19921875
- reward: bfloat16 [6, 12288], P(None, 'bel'), may hold values from -1.796875 to 1.796875
- belief_index: int32 [128, 6, 48], P('bel'), may hold values from 0 to 511
- action: int32 [128], replicated, may hold values from 0 to 5
Outputs:
- new_alphas: bfloat16 [128, 12288], P('st', 'bel')
The draws below stay inside these ranges and needn't reach their ends.
Inputs may be any that keep to these rules, and one draw needn't show every extreme that they name: `belief_index`: indices of rows of alphas.
All inputs are finite; a program needn't handle non-finite values.
Results may differ from the reference program's by a relative error of at most 0.0044.
Values may be sent and summed in bfloat16 or wider, within the bound.
A program may use at most 128 MiB of HBM per device.

```python
import math
import jax
import jax.numpy as jnp
from jax import lax

S = 12288
ACTS = 6
O = 48
K = 512
BELIEFS = 128


def with_ends(values, rng, low, largest):
    index_at = [jax.random.randint(jax.random.fold_in(rng, axis), (), 0, length) for axis, length in enumerate(values.shape)]
    main_axis = values.shape.index(max(values.shape))
    neighbour = index_at[:main_axis] + [(index_at[main_axis] + 1) % values.shape[main_axis]] + index_at[main_axis + 1:]
    return values.at[tuple(index_at)].set(low).at[tuple(neighbour)].set(largest)


def block_scale(stream_key, extent, shards, smallest, high):
    loudness, own = 1.0, jax.random.fold_in(stream_key, 6)
    for dim, blocks in shards:
        heights = jnp.exp(jax.random.uniform(jax.random.fold_in(own, dim), (blocks,), jnp.float32, smallest / len(shards), high / len(shards)))
        loudness = loudness * jnp.repeat(heights, extent[dim] // blocks).reshape([-1 if axis == dim else 1 for axis in range(len(extent))])
    return loudness


def gaussian(stream_key, dims, width, most, shards=(), kind=jnp.bfloat16):
    drawn = jax.random.normal(stream_key, dims, jnp.float32) * width
    if len(shards) > 0:
        drawn = block_scale(stream_key, dims, shards, -0.22, 0.18) * drawn
    return jnp.clip(drawn, min=-most, max=most).astype(kind)


def setup_inputs(seed: int = 0) -> dict:
    seeds = jax.random.split(jax.random.key(seed), 7)
    alphas = gaussian(seeds[0], (K, S), 20.0, 120.0, ((1, 4),))
    transitions = jnp.clip(jnp.exp(math.log(10.0) - 9.21089 * jax.random.uniform(seeds[1], (ACTS, S, S), jnp.float32) ** block_scale(seeds[1], (ACTS, S, S), ((1, 8), (2, 4)), -0.2, 0.2)), 0.0009994507, 10.0).astype(jnp.bfloat16)
    observe = jnp.clip(jnp.exp(math.log(0.19921875) - 4.6018058 * jax.random.uniform(seeds[2], (ACTS, O, S), jnp.float32) ** block_scale(seeds[2], (ACTS, O, S), ((2, 4),), -0.2, 0.2)), 0.0019989014, 0.19921875).astype(jnp.bfloat16)
    reward = gaussian(seeds[3], (ACTS, S), 0.3, 1.796875, ((1, 8),))
    belief_index = with_ends(jax.random.randint(seeds[4], (BELIEFS, ACTS, O), 0, K), jax.random.fold_in(seeds[4], 1), 0, K - 1).astype(jnp.int32)
    action = with_ends(jax.random.randint(seeds[5], (BELIEFS,), 0, ACTS), jax.random.fold_in(seeds[5], 1), 0, ACTS - 1).astype(jnp.int32)
    return dict(alphas=alphas, transitions=transitions, observe=observe, reward=reward, belief_index=belief_index, action=action)


discount = 0.95


def mixture_block(alphas, observe, index_rows, action_rows):
    onehot = action_rows[:, None] == jnp.arange(ACTS, dtype=jnp.int32)[None, :]
    chosen = jnp.sum(jnp.where(onehot[:, :, None], index_rows, 0), axis=1).astype(jnp.int32)
    picked = alphas[chosen].astype(jnp.float32)
    weights = observe[action_rows].astype(jnp.float32)
    return jnp.sum(picked * weights, axis=1).astype(jnp.bfloat16)


def grouped_product(rows, acts, weights, block):
    count = rows.shape[0]
    kinds = weights.shape[0]
    blocks = count // block + kinds - 1
    onehot = (acts[:, None] == jnp.arange(kinds, dtype=jnp.int32)[None, :]).astype(jnp.int32)
    totals = jnp.sum(onehot, axis=0).astype(jnp.int32)
    filled = ((totals + block - 1) // block).astype(jnp.int32)
    ends = jnp.cumsum(filled).astype(jnp.int32)
    starts = (ends - filled).astype(jnp.int32)
    before = (jnp.cumsum(onehot, axis=0).astype(jnp.int32) - onehot).astype(jnp.int32)
    rank = jnp.sum(before * onehot, axis=1).astype(jnp.int32)
    first = jnp.sum(onehot * starts[None, :], axis=1).astype(jnp.int32)
    target = (first * block + rank).astype(jnp.int32)
    source = jnp.zeros((blocks * block,), jnp.int32).at[target].set(jnp.arange(count, dtype=jnp.int32))
    padded = rows[source].reshape(blocks, block, rows.shape[1])
    owner = jnp.sum((jnp.arange(blocks, dtype=jnp.int32)[:, None] >= ends[None, :]).astype(jnp.int32), axis=1)
    owner = jnp.minimum(owner, kinds - 1).astype(jnp.int32)

    def one_block(pair):
        part, which = pair
        matrix = lax.dynamic_index_in_dim(weights, which, 0, keepdims=False)
        return lax.dot_general(part, matrix, (((1,), (1,)), ((), ())), preferred_element_type=jnp.float32)

    result = lax.map(one_block, (padded, owner)).reshape(blocks * block, weights.shape[1])
    return result[target]


def reference(alphas, transitions, observe, reward, belief_index, action):
    beliefs = belief_index.shape[0]
    block = math.gcd(beliefs, 64)
    index_blocks = belief_index.reshape(beliefs // block, block, ACTS, O)
    action_blocks = action.reshape(beliefs // block, block)
    mixture = lax.map(lambda pair: mixture_block(alphas, observe, pair[0], pair[1]), (index_blocks, action_blocks))
    mixture = mixture.reshape(beliefs, S)
    carried = grouped_product(mixture, action, transitions, math.gcd(beliefs, 256))
    gained = reward[action].astype(jnp.float32)
    return (gained + (discount / S) * carried).astype(jnp.bfloat16)
```

```python
import functools
import math

import jax
import jax.numpy as jnp
from jax import lax
from jax.experimental import pallas as pl
from jax.experimental.pallas import tpu as pltpu
from jax.sharding import PartitionSpec as P

discount = 0.95
MESH = pl.DeviceIdType.MESH
VMEM_BYTES = 67_043_328
UNIT = 256
PHASES = 4


def kernel(
    n_bel,
    n_st,
    scale,
    n_ph,
    nb,
    tail,
    act_h,
    act_row_h,
    bi_h,
    reward_h,
    alphas_h,
    obs_h,
    w_h,
    out_h,
    act_s,
    act_row,
    bi,
    reward,
    spare,
    obs_v,
    w_v,
    onehot,
    act_col,
    mixf,
    mix,
    acc,
    terms,
    recv,
    out_v,
    in_sem,
    ao_sem,
    w_sem,
    out_sem,
    ag_send,
    ag_recv,
    rs_send,
    rs_recv,
):
    acts, own, obs = bi.shape
    k_rows = alphas_h.shape[0]
    beliefs, depth = mix.shape
    states = w_v.shape[1]
    out_rows = out_v.shape[0]
    block = act_row.shape[1]
    kw = depth // n_ph
    nj = states // nb
    fits = states >= k_rows
    alphas_v = w_v.at[acts - 1, states - k_rows :, :] if fits else spare
    early = nj - 1 if n_ph > 1 else 0
    head = max(n_ph - 2, 0)
    blocks = [(j * nb, nb) for j in range(early)]
    blocks += [(lo, tail) for lo in range(early * nb, states, tail)]

    me = lax.axis_index("bel")
    st = lax.axis_index("st")

    barrier = pltpu.get_barrier_semaphore()
    for d in range(1, n_bel):
        pl.semaphore_signal(
            barrier, inc=1, device_id={"bel": lax.rem(me + d, n_bel)}, device_id_type=MESH
        )
    for d in range(1, n_st):
        pl.semaphore_signal(
            barrier, inc=1, device_id={"st": lax.rem(st + d, n_st)}, device_id_type=MESH
        )

    small = [
        pltpu.make_async_copy(src, dst, in_sem.at[i])
        for i, (src, dst) in enumerate(
            ((act_h, act_s), (bi_h, bi), (act_row_h, act_row), (reward_h, reward))
        )
    ]

    def cols_of(c):
        if n_ph == 1:
            return pl.ds(0, depth)
        return pl.ds(pl.multiple_of(c * kw, kw), kw)

    def load_alphas(c):
        return pltpu.make_async_copy(
            alphas_h.at[:, cols_of(c)], alphas_v.at[:, cols_of(c)], ao_sem.at[0, c]
        )

    def load_obs(c):
        return pltpu.make_async_copy(
            obs_h.at[:, :, cols_of(c)], obs_v.at[:, :, cols_of(c)], ao_sem.at[1, c]
        )

    def load_w(p, j, a):
        rows = pl.ds(pl.multiple_of(j * nb, nb), nb)
        return pltpu.make_async_copy(
            w_h.at[a, rows, cols_of(p)], w_v.at[a, rows, cols_of(p)], w_sem.at[p, j, a]
        )

    def shared(j, a):
        return fits and a == acts - 1 and (j + 1) * nb > states - k_rows

    def issue_w(p, late=None):
        for j in range(nj):
            for a in range(acts):
                if late is None or shared(j, a) == late:
                    load_w(p, j, a).start()

    def await_w(p, j):
        for a in range(acts):
            load_w(p, j, a).wait()

    for copy in small:
        copy.start()
    for c in range(n_ph):
        load_alphas(c).start()
        load_obs(c).start()

    for copy in small:
        copy.wait()

    eye = lax.broadcasted_iota(jnp.int32, (block, block), 0) == lax.broadcasted_iota(
        jnp.int32, (block, block), 1
    )
    for r in range(beliefs // block):
        row = act_row[r : r + 1, :].astype(jnp.float32)
        act_col[r * block : (r + 1) * block, :] = jnp.sum(
            jnp.where(eye, row, 0.0), axis=1, keepdims=True
        )
    eye_o = lax.broadcasted_iota(jnp.int32, (obs, obs), 0) == lax.broadcasted_iota(
        jnp.int32, (obs, obs), 1
    )
    lanes = lax.broadcasted_iota(jnp.int32, (obs, k_rows), 1).astype(jnp.float32)
    for i in range(own):
        a = act_s[me * own + i]
        row = bi[pl.ds(a, 1), i, :].astype(jnp.float32)
        col = jnp.sum(jnp.where(eye_o, row, 0.0), axis=1, keepdims=True)
        onehot[i * obs : (i + 1) * obs, :] = jnp.where(lanes == col, 1.0, 0.0).astype(jnp.bfloat16)

    mine_rows = pl.ds(pl.multiple_of(me * own, own), own)

    unit = mixf.shape[1]

    def mixture(c):
        def one_unit(u, carry):
            cols = pl.ds(pl.multiple_of(c * kw + u * unit, unit), unit)
            picked = jnp.dot(
                onehot[...], alphas_v[:, cols], preferred_element_type=jnp.float32
            )
            for i in range(own):
                a = act_s[me * own + i]
                weights = obs_v[a, :, cols].astype(jnp.float32)
                part = picked[i * obs : (i + 1) * obs, :] * weights
                mixf[i : i + 1, :] = jnp.sum(part, axis=0, keepdims=True)
            mix[mine_rows, cols] = mixf[...].astype(jnp.bfloat16)
            return carry

        lax.fori_loop(0, kw // unit, one_unit, 0)

    def send(c, d, src, dst):
        piece = mix.at[pl.ds(pl.multiple_of(src * own, own), own), cols_of(c)]
        return pltpu.make_async_remote_copy(
            src_ref=piece,
            dst_ref=piece,
            send_sem=ag_send.at[c, d - 1],
            recv_sem=ag_recv.at[c, d - 1],
            device_id={"bel": dst},
            device_id_type=MESH,
        )

    def each_peer(fn):
        def step(i, carry):
            fn(n_bel - 1 - i)
            return carry

        lax.fori_loop(0, n_bel - 1, step, 0, unroll=n_bel <= 8)

    for c in range(n_ph):
        load_alphas(c).wait()
        load_obs(c).wait()
    issue_w(0, False)
    pl.semaphore_wait(barrier, n_bel - 1 + n_st - 1)

    def one_chunk(c, carry):
        mixture(c)

        def push(d):
            send(c, d, me, lax.rem(me + d, n_bel)).start()

        each_peer(push)
        return carry

    lax.fori_loop(0, n_ph, one_chunk, 0)
    issue_w(0, True)
    if n_ph > 1:
        issue_w(1)

    def arrive(c):
        def take(d):
            send(c, d, lax.rem(me - d + n_bel, n_bel), lax.rem(me + d, n_bel)).wait_recv()

        each_peer(take)

    def rs_copy(lo, size, k, d):
        peer = lax.rem(st + d, n_st)
        cols = pl.ds(pl.multiple_of(lo, tail), size)
        return pltpu.make_async_remote_copy(
            src_ref=terms.at[pl.ds(pl.multiple_of(peer * out_rows, out_rows), out_rows), cols],
            dst_ref=recv.at[d - 1, :, cols],
            send_sem=rs_send.at[k, d - 1],
            recv_sem=rs_recv.at[k, d - 1],
            device_id={"st": peer},
            device_id_type=MESH,
        )

    def product(a, rows, cols, r):
        part = slice(r * block, (r + 1) * block)
        keep = jnp.where(act_col[part, :] == float(a), 1.0, 0.0).astype(jnp.bfloat16)
        return lax.dot_general(
            w_v[a, rows, cols],
            mix[part, cols] * keep,
            (((1,), (1,)), ((), ())),
            preferred_element_type=jnp.float32,
        )

    def products(rows, cols, r):
        total = product(0, rows, cols, r)
        for a in range(1, acts):
            total += product(a, rows, cols, r)
        return total

    def finish(lo, size, k, cols, add):
        rows = pl.ds(pl.multiple_of(lo, tail), size)
        for r in range(beliefs // block):
            total = products(rows, cols, r)
            if add:
                total += acc[r, rows, :]
            terms[r * block : (r + 1) * block, rows] = total.T
        for d in range(1, n_st):
            rs_copy(lo, size, k, d).start()

    if n_ph > 1:

        def partial(i, carry):
            p, j = i // nj, lax.rem(i, nj)

            @pl.when(j == 0)
            def _():
                arrive(p)

            await_w(p, j)
            rows = pl.ds(pl.multiple_of(j * nb, nb), nb)
            for r in range(beliefs // block):
                total = products(rows, cols_of(p), r)
                acc[r, rows, :] = jnp.where(p == 0, total, acc[r, rows, :] + total)
            for q in range(2, n_ph):

                @pl.when(i == (q - 2) * nj)
                def _():
                    issue_w(q)

            return carry

        lax.fori_loop(0, head * nj + early, partial, 0)
        if early == 0:
            arrive(n_ph - 2)
        arrive(n_ph - 1)

        def whole_block(j, carry):
            await_w(n_ph - 1, j)
            finish(j * nb, nb, j, cols_of(n_ph - 1), True)
            return carry

        lax.fori_loop(0, early, whole_block, 0)
        await_w(n_ph - 2, nj - 1)
        await_w(n_ph - 1, nj - 1)
    else:
        arrive(0)
        for j in range(nj):
            await_w(0, j)

    def tail_block(t, carry):
        left = slice(head * kw, depth)
        finish(early * nb + t * tail, tail, early + t, left, head > 0)
        return carry

    lax.fori_loop(0, (states - early * nb) // tail, tail_block, 0)

    mine = pl.ds(pl.multiple_of(st * out_rows, out_rows), out_rows)
    which = act_col[mine, :]

    def write_out(k):
        lo, size = blocks[k]
        return pltpu.make_async_copy(
            out_v.at[:, pl.ds(lo, size)], out_h.at[:, pl.ds(lo, size)], out_sem.at[k]
        )

    for k, (lo, size) in enumerate(blocks):
        cols = slice(lo, lo + size)
        gained = jnp.zeros((out_rows, size), jnp.float32)
        for a in range(acts):
            gained += jnp.where(
                which == float(a), reward[a : a + 1, cols].astype(jnp.float32), 0.0
            )
        total = terms[mine, cols]
        for d in range(1, n_st):
            rs_copy(lo, size, k, d).wait_recv()
            total += recv[d - 1, :, cols]
        out_v[:, cols] = (gained + scale * total).astype(out_v.dtype)
        write_out(k).start()

    for c in range(n_ph):

        def sent(d, c=c):
            send(c, d, me, lax.rem(me + d, n_bel)).wait_send()

        each_peer(sent)
    for k, (lo, size) in enumerate(blocks):
        for d in range(1, n_st):
            rs_copy(lo, size, k, d).wait_send()
    for k in range(len(blocks)):
        write_out(k).wait()


def body(n_bel, n_st, alphas, transitions, observe, reward, belief_index, action):
    k_rows, depth = alphas.shape
    acts, states, _ = transitions.shape
    obs = observe.shape[1]
    own = belief_index.shape[0]
    beliefs = action.shape[0]
    out_rows = beliefs // n_st
    block = math.gcd(beliefs, 128)
    nb = math.gcd(states, 512) if states % 128 == 0 else states
    tail = nb // 2 if nb % 256 == 0 else nb
    nj = states // nb
    n_ph = PHASES if depth % (PHASES * 128) == 0 else 1
    kw = depth // n_ph
    unit = UNIT if kw % UNIT == 0 else kw
    n_blocks = (nj - 1 + nb // tail) if n_ph > 1 else states // tail
    scale = discount / (depth * n_st)
    hbm = pl.BlockSpec(memory_space=pl.ANY)
    return pl.pallas_call(
        functools.partial(kernel, n_bel, n_st, scale, n_ph, nb, tail),
        out_shape=jax.ShapeDtypeStruct((out_rows, states), jnp.bfloat16),
        in_specs=[hbm] * 7,
        out_specs=hbm,
        scratch_shapes=[
            pltpu.SMEM((beliefs,), jnp.int32),
            pltpu.VMEM((beliefs // block, block), jnp.int32),
            pltpu.VMEM((acts, own, obs), jnp.int32),
            pltpu.VMEM((acts, states), jnp.bfloat16),
            pltpu.VMEM((16, 128) if states >= k_rows else (k_rows, depth), jnp.bfloat16),
            pltpu.VMEM((acts, obs, depth), jnp.bfloat16),
            pltpu.VMEM((acts, states, depth), jnp.bfloat16),
            pltpu.VMEM((own * obs, k_rows), jnp.bfloat16),
            pltpu.VMEM((beliefs, 1), jnp.float32),
            pltpu.VMEM((own, unit), jnp.float32),
            pltpu.VMEM((beliefs, depth), jnp.bfloat16),
            pltpu.VMEM((beliefs // block, states, block), jnp.float32),
            pltpu.VMEM((beliefs, states), jnp.float32),
            pltpu.VMEM((n_st - 1, out_rows, states), jnp.float32),
            pltpu.VMEM((out_rows, states), jnp.bfloat16),
            pltpu.SemaphoreType.DMA((4,)),
            pltpu.SemaphoreType.DMA((2, n_ph)),
            pltpu.SemaphoreType.DMA((n_ph, nj, acts)),
            pltpu.SemaphoreType.DMA((n_blocks,)),
            pltpu.SemaphoreType.DMA((n_ph, n_bel - 1)),
            pltpu.SemaphoreType.DMA((n_ph, n_bel - 1)),
            pltpu.SemaphoreType.DMA((n_blocks, n_st - 1)),
            pltpu.SemaphoreType.DMA((n_blocks, n_st - 1)),
        ],
        compiler_params=pltpu.CompilerParams(
            collective_id=0, has_side_effects=True, vmem_limit_bytes=VMEM_BYTES
        ),
    )(
        action,
        action.reshape(beliefs // block, block),
        belief_index.transpose(1, 0, 2),
        reward,
        alphas,
        observe,
        transitions,
    )


def solution(mesh):
    placed = (
        P(None, "st"),
        P(None, "bel", "st"),
        P(None, None, "st"),
        P(None, "bel"),
        P("bel", None, None),
        P(),
    )
    return jax.shard_map(
        functools.partial(body, mesh.shape["bel"], mesh.shape["st"]),
        mesh=mesh,
        in_specs=placed,
        out_specs=P("st", "bel"),
        check_vma=False,
    )
```

```python
import functools
import math

import jax
import jax.numpy as jnp
from jax import lax
from jax.experimental import pallas as pl
from jax.experimental.pallas import tpu as pltpu
from jax.sharding import PartitionSpec as P

discount = 0.95
MESH = pl.DeviceIdType.MESH
VMEM_BYTES = 67_043_328
UNIT = 256
PHASES = 4
AHEAD = 1
PUSHES = (0, 0, 0, 2)


def kernel(
    n_bel,
    n_st,
    scale,
    n_ph,
    nb,
    tail,
    act_h,
    act_row_h,
    bi_h,
    reward_h,
    alphas_h,
    obs_h,
    w_h,
    out_h,
    act_s,
    act_row,
    bi,
    reward,
    spare,
    obs_v,
    w_v,
    onehot,
    act_col,
    mixf,
    mix,
    acc,
    terms,
    recv,
    out_v,
    in_sem,
    ao_sem,
    w_sem,
    out_sem,
    ag_send,
    ag_recv,
    rs_send,
    rs_recv,
):
    acts, own, obs = bi.shape
    k_rows = alphas_h.shape[0]
    beliefs, depth = mix.shape
    states = w_v.shape[1]
    out_rows = out_v.shape[0]
    block = act_row.shape[1]
    kw = depth // n_ph
    nj = states // nb
    fits = states >= k_rows
    alphas_v = w_v.at[acts - 1, states - k_rows :, :] if fits else spare
    early = nj - 1 if n_ph > 1 else 0
    head = max(n_ph - 2, 0)
    blocks = [(j * nb, nb) for j in range(early)]
    blocks += [(lo, tail) for lo in range(early * nb, states, tail)]

    me = lax.axis_index("bel")
    st = lax.axis_index("st")

    barrier = pltpu.get_barrier_semaphore()
    for d in range(1, n_bel):
        pl.semaphore_signal(
            barrier, inc=1, device_id={"bel": lax.rem(me + d, n_bel)}, device_id_type=MESH
        )
    for d in range(1, n_st):
        pl.semaphore_signal(
            barrier, inc=1, device_id={"st": lax.rem(st + d, n_st)}, device_id_type=MESH
        )

    small = [
        pltpu.make_async_copy(src, dst, in_sem.at[i])
        for i, (src, dst) in enumerate(
            ((act_h, act_s), (bi_h, bi), (act_row_h, act_row), (reward_h, reward))
        )
    ]

    def cols_of(c):
        if n_ph == 1:
            return pl.ds(0, depth)
        return pl.ds(pl.multiple_of(c * kw, kw), kw)

    def load_alphas(c):
        return pltpu.make_async_copy(
            alphas_h.at[:, cols_of(c)], alphas_v.at[:, cols_of(c)], ao_sem.at[c]
        )

    load_obs = pltpu.make_async_copy(obs_h, obs_v, ao_sem.at[n_ph])

    def load_w(p, j, a):
        rows = pl.ds(pl.multiple_of(j * nb, nb), nb)
        return pltpu.make_async_copy(
            w_h.at[a, rows, cols_of(p)], w_v.at[a, rows, cols_of(p)], w_sem.at[p, j, a]
        )

    def shared(j, a):
        return fits and a == acts - 1 and (j + 1) * nb > states - k_rows

    def issue_w(p, late=None):
        for j in range(nj):
            for a in range(acts):
                if late is None or shared(j, a) == late:
                    load_w(p, j, a).start()

    def await_w(p, j):
        for a in range(acts):
            load_w(p, j, a).wait()

    for copy in small:
        copy.start()
    load_alphas(0).start()
    load_obs.start()

    for copy in small:
        copy.wait()

    eye = lax.broadcasted_iota(jnp.int32, (block, block), 0) == lax.broadcasted_iota(
        jnp.int32, (block, block), 1
    )
    for r in range(beliefs // block):
        row = act_row[r : r + 1, :].astype(jnp.float32)
        act_col[r * block : (r + 1) * block, :] = jnp.sum(
            jnp.where(eye, row, 0.0), axis=1, keepdims=True
        )
    eye_o = lax.broadcasted_iota(jnp.int32, (obs, obs), 0) == lax.broadcasted_iota(
        jnp.int32, (obs, obs), 1
    )
    lanes = lax.broadcasted_iota(jnp.int32, (obs, k_rows), 1).astype(jnp.float32)
    for i in range(own):
        a = act_s[me * own + i]
        row = bi[pl.ds(a, 1), i, :].astype(jnp.float32)
        col = jnp.sum(jnp.where(eye_o, row, 0.0), axis=1, keepdims=True)
        onehot[i * obs : (i + 1) * obs, :] = jnp.where(lanes == col, 1.0, 0.0).astype(jnp.bfloat16)

    mine_rows = pl.ds(pl.multiple_of(me * own, own), own)

    unit = mixf.shape[1]

    def mixture(c):
        def one_unit(u, carry):
            cols = pl.ds(pl.multiple_of(c * kw + u * unit, unit), unit)
            picked = jnp.dot(
                onehot[...], alphas_v[:, cols], preferred_element_type=jnp.float32
            )
            for i in range(own):
                a = act_s[me * own + i]
                weights = obs_v[a, :, cols].astype(jnp.float32)
                part = picked[i * obs : (i + 1) * obs, :] * weights
                mixf[i : i + 1, :] = jnp.sum(part, axis=0, keepdims=True)
            mix[mine_rows, cols] = mixf[...].astype(jnp.bfloat16)
            return carry

        lax.fori_loop(0, kw // unit, one_unit, 0)

    def send(c, d, src, dst):
        piece = mix.at[pl.ds(pl.multiple_of(src * own, own), own), cols_of(c)]
        return pltpu.make_async_remote_copy(
            src_ref=piece,
            dst_ref=piece,
            send_sem=ag_send.at[c],
            recv_sem=ag_recv.at[c],
            device_id={"bel": dst},
            device_id_type=MESH,
        )

    def each_peer(fn):
        def step(i, carry):
            fn(n_bel - 1 - i)
            return carry

        lax.fori_loop(0, n_bel - 1, step, 0, unroll=n_bel <= 8)

    ahead = min(AHEAD, n_ph)

    def push(c):
        each_peer(lambda d: send(c, d, me, lax.rem(me + d, n_bel)).start())

    def one_chunk(c, carry):
        load_alphas(c).wait()

        @pl.when(c == 0)
        def _():
            for later in range(1, n_ph):
                load_alphas(later).start()
            load_obs.wait()

        mixture(c)

        @pl.when(c == ahead - 1)
        def _():
            issue_w(0, False)
            pl.semaphore_wait(barrier, n_bel - 1 + n_st - 1)
            push(0)

        return carry

    lax.fori_loop(0, n_ph, one_chunk, 0)
    issue_w(0, True)
    if n_ph > 1:
        push(1)
        issue_w(1)

    def others(c, sem):
        piece = mix.at[pl.ds(0, beliefs - own), cols_of(c)]
        return pltpu.make_async_copy(piece, piece, sem.at[c])

    def arrive(c):
        others(c, ag_recv).wait()

    def rs_copy(lo, size, k, d):
        peer = lax.rem(st + d, n_st)
        cols = pl.ds(pl.multiple_of(lo, tail), size)
        return pltpu.make_async_remote_copy(
            src_ref=terms.at[pl.ds(pl.multiple_of(peer * out_rows, out_rows), out_rows), cols],
            dst_ref=recv.at[d - 1, :, cols],
            send_sem=rs_send.at[k],
            recv_sem=rs_recv.at[k],
            device_id={"st": peer},
            device_id_type=MESH,
        )

    def product(a, rows, cols, r):
        part = slice(r * block, (r + 1) * block)
        keep = jnp.where(act_col[part, :] == float(a), 1.0, 0.0).astype(jnp.bfloat16)
        return lax.dot_general(
            w_v[a, rows, cols],
            mix[part, cols] * keep,
            (((1,), (1,)), ((), ())),
            preferred_element_type=jnp.float32,
        )

    def products(rows, cols, r):
        total = product(0, rows, cols, r)
        for a in range(1, acts):
            total += product(a, rows, cols, r)
        return total

    def finish(lo, size, k, cols, add):
        rows = pl.ds(pl.multiple_of(lo, tail), size)
        for r in range(beliefs // block):
            total = products(rows, cols, r)
            if add:
                total += acc[r, rows, :]
            terms[r * block : (r + 1) * block, rows] = total.T
        for d in range(1, n_st):
            rs_copy(lo, size, k, d).start()

    if n_ph > 1:

        def partial(i, carry):
            p, j = i // nj, lax.rem(i, nj)

            @pl.when(j == 0)
            def _():
                arrive(p)

            for c in range(2, n_ph):

                @pl.when(i == PUSHES[c])
                def _(c=c):
                    push(c)

            await_w(p, j)
            rows = pl.ds(pl.multiple_of(j * nb, nb), nb)
            for r in range(beliefs // block):
                total = products(rows, cols_of(p), r)
                acc[r, rows, :] = jnp.where(p == 0, total, acc[r, rows, :] + total)
            for q in range(2, n_ph):

                @pl.when(i == (q - 2) * nj)
                def _():
                    issue_w(q)

            return carry

        lax.fori_loop(0, head * nj + early, partial, 0)
        if early == 0:
            arrive(n_ph - 2)
        arrive(n_ph - 1)

        def whole_block(j, carry):
            await_w(n_ph - 1, j)
            finish(j * nb, nb, j, cols_of(n_ph - 1), True)
            return carry

        lax.fori_loop(0, early, whole_block, 0)
        await_w(n_ph - 2, nj - 1)
        await_w(n_ph - 1, nj - 1)
    else:
        arrive(0)
        for j in range(nj):
            await_w(0, j)

    def tail_block(t, carry):
        left = slice(head * kw, depth)
        finish(early * nb + t * tail, tail, early + t, left, head > 0)
        return carry

    lax.fori_loop(0, (states - early * nb) // tail, tail_block, 0)

    mine = pl.ds(pl.multiple_of(st * out_rows, out_rows), out_rows)
    which = act_col[mine, :]

    for c in range(n_ph):
        others(c, ag_send).wait()

    def pieces(k, sem):
        lo, size = blocks[k]
        part = recv.at[:, :, pl.ds(lo, size)]
        return pltpu.make_async_copy(part, part, sem.at[k])

    def write_out(k):
        lo, size = blocks[k]
        return pltpu.make_async_copy(
            out_v.at[:, pl.ds(lo, size)], out_h.at[:, pl.ds(lo, size)], out_sem.at[k]
        )

    for k, (lo, size) in enumerate(blocks):
        cols = slice(lo, lo + size)
        gained = jnp.zeros((out_rows, size), jnp.float32)
        for a in range(acts):
            gained += jnp.where(
                which == float(a), reward[a : a + 1, cols].astype(jnp.float32), 0.0
            )
        total = terms[mine, cols]
        pieces(k, rs_recv).wait()
        for d in range(1, n_st):
            total += recv[d - 1, :, cols]
        out_v[:, cols] = (gained + scale * total).astype(out_v.dtype)
        write_out(k).start()

    for k in range(len(blocks)):
        pieces(k, rs_send).wait()
    for k in range(len(blocks)):
        write_out(k).wait()


def body(n_bel, n_st, alphas, transitions, observe, reward, belief_index, action):
    k_rows, depth = alphas.shape
    acts, states, _ = transitions.shape
    obs = observe.shape[1]
    own = belief_index.shape[0]
    beliefs = action.shape[0]
    out_rows = beliefs // n_st
    block = math.gcd(beliefs, 128)
    nb = math.gcd(states, 768) if states % 128 == 0 else states
    tail = math.gcd(nb, 256) if nb % 128 == 0 else nb
    nj = states // nb
    n_ph = PHASES if depth % (PHASES * 128) == 0 else 1
    kw = depth // n_ph
    unit = UNIT if kw % UNIT == 0 else kw
    n_blocks = (nj - 1 + nb // tail) if n_ph > 1 else states // tail
    scale = discount / (depth * n_st)
    hbm = pl.BlockSpec(memory_space=pl.ANY)
    return pl.pallas_call(
        functools.partial(kernel, n_bel, n_st, scale, n_ph, nb, tail),
        out_shape=jax.ShapeDtypeStruct((out_rows, states), jnp.bfloat16),
        in_specs=[hbm] * 7,
        out_specs=hbm,
        scratch_shapes=[
            pltpu.SMEM((beliefs,), jnp.int32),
            pltpu.VMEM((beliefs // block, block), jnp.int32),
            pltpu.VMEM((acts, own, obs), jnp.int32),
            pltpu.VMEM((acts, states), jnp.bfloat16),
            pltpu.VMEM((16, 128) if states >= k_rows else (k_rows, depth), jnp.bfloat16),
            pltpu.VMEM((acts, obs, depth), jnp.bfloat16),
            pltpu.VMEM((acts, states, depth), jnp.bfloat16),
            pltpu.VMEM((own * obs, k_rows), jnp.bfloat16),
            pltpu.VMEM((beliefs, 1), jnp.float32),
            pltpu.VMEM((own, unit), jnp.float32),
            pltpu.VMEM((beliefs, depth), jnp.bfloat16),
            pltpu.VMEM((beliefs // block, states, block), jnp.float32),
            pltpu.VMEM((beliefs, states), jnp.float32),
            pltpu.VMEM((n_st - 1, out_rows, states), jnp.float32),
            pltpu.VMEM((out_rows, states), jnp.bfloat16),
            pltpu.SemaphoreType.DMA((4,)),
            pltpu.SemaphoreType.DMA((n_ph + 1,)),
            pltpu.SemaphoreType.DMA((n_ph, nj, acts)),
            pltpu.SemaphoreType.DMA((n_blocks,)),
            pltpu.SemaphoreType.DMA((n_ph,)),
            pltpu.SemaphoreType.DMA((n_ph,)),
            pltpu.SemaphoreType.DMA((n_blocks,)),
            pltpu.SemaphoreType.DMA((n_blocks,)),
        ],
        compiler_params=pltpu.CompilerParams(
            collective_id=0, has_side_effects=True, vmem_limit_bytes=VMEM_BYTES
        ),
    )(
        action,
        action.reshape(beliefs // block, block),
        belief_index.transpose(1, 0, 2),
        reward,
        alphas,
        observe,
        transitions,
    )


def solution(mesh):
    placed = (
        P(None, "st"),
        P(None, "bel", "st"),
        P(None, None, "st"),
        P(None, "bel"),
        P("bel", None, None),
        P(),
    )
    return jax.shard_map(
        functools.partial(body, mesh.shape["bel"], mesh.shape["st"]),
        mesh=mesh,
        in_specs=placed,
        out_specs=P("st", "bel"),
        check_vma=False,
    )
```

```python
import functools
import math

import jax
import jax.numpy as jnp
from jax import lax
from jax.experimental import pallas as pl
from jax.experimental.pallas import tpu as pltpu
from jax.sharding import PartitionSpec as P

discount = 0.95
MESH = pl.DeviceIdType.MESH
VMEM_BYTES = 67_043_328
UNIT = 256
PHASES = 4
AHEAD = 1
PUSHES = (0, 0, 0, 0)
RELAYS = (0, 0, 1, 2)
DIRECT = 1


def kernel(
    n_bel,
    n_st,
    scale,
    n_ph,
    nb,
    tail,
    act_h,
    act_row_h,
    bi_h,
    reward_h,
    alphas_h,
    obs_h,
    w_h,
    out_h,
    act_s,
    act_row,
    bi,
    reward,
    spare,
    obs_v,
    w_v,
    onehot,
    act_col,
    mixf,
    mix,
    acc,
    terms,
    recv,
    out_v,
    in_sem,
    ao_sem,
    w_sem,
    out_sem,
    ag_send,
    ag_recv,
    ag_far,
    rs_send,
    rs_recv,
):
    acts, own, obs = bi.shape
    k_rows = alphas_h.shape[0]
    beliefs, depth = mix.shape
    states = w_v.shape[1]
    out_rows = out_v.shape[0]
    block = act_row.shape[1]
    kw = depth // n_ph
    nj = states // nb
    fits = states >= k_rows
    alphas_v = w_v.at[acts - 1, states - k_rows :, :] if fits else spare
    early = nj - 1 if n_ph > 1 else 0
    head = max(n_ph - 2, 0)
    blocks = [(j * nb, nb) for j in range(early)]
    blocks += [(lo, tail) for lo in range(early * nb, states, tail)]

    me = lax.axis_index("bel")
    st = lax.axis_index("st")

    barrier = pltpu.get_barrier_semaphore()
    for d in range(1, n_bel):
        pl.semaphore_signal(
            barrier, inc=1, device_id={"bel": lax.rem(me + d, n_bel)}, device_id_type=MESH
        )
    for d in range(1, n_st):
        pl.semaphore_signal(
            barrier, inc=1, device_id={"st": lax.rem(st + d, n_st)}, device_id_type=MESH
        )

    small = [
        pltpu.make_async_copy(src, dst, in_sem.at[i])
        for i, (src, dst) in enumerate(
            ((act_h, act_s), (bi_h, bi), (act_row_h, act_row), (reward_h, reward))
        )
    ]

    def cols_of(c):
        if n_ph == 1:
            return pl.ds(0, depth)
        return pl.ds(pl.multiple_of(c * kw, kw), kw)

    def load_alphas(c):
        return pltpu.make_async_copy(
            alphas_h.at[:, cols_of(c)], alphas_v.at[:, cols_of(c)], ao_sem.at[c]
        )

    load_obs = pltpu.make_async_copy(obs_h, obs_v, ao_sem.at[n_ph])

    def load_w(p, j, a):
        rows = pl.ds(pl.multiple_of(j * nb, nb), nb)
        return pltpu.make_async_copy(
            w_h.at[a, rows, cols_of(p)], w_v.at[a, rows, cols_of(p)], w_sem.at[p, j, a]
        )

    def shared(j, a):
        return fits and a == acts - 1 and (j + 1) * nb > states - k_rows

    def issue_w(p, late=None):
        for j in range(nj):
            for a in range(acts):
                if late is None or shared(j, a) == late:
                    load_w(p, j, a).start()

    def await_w(p, j):
        for a in range(acts):
            load_w(p, j, a).wait()

    for copy in small:
        copy.start()
    load_alphas(0).start()
    load_obs.start()

    for copy in small:
        copy.wait()

    eye = lax.broadcasted_iota(jnp.int32, (block, block), 0) == lax.broadcasted_iota(
        jnp.int32, (block, block), 1
    )
    for r in range(beliefs // block):
        row = act_row[r : r + 1, :].astype(jnp.float32)
        act_col[r * block : (r + 1) * block, :] = jnp.sum(
            jnp.where(eye, row, 0.0), axis=1, keepdims=True
        )
    eye_o = lax.broadcasted_iota(jnp.int32, (obs, obs), 0) == lax.broadcasted_iota(
        jnp.int32, (obs, obs), 1
    )
    lanes = lax.broadcasted_iota(jnp.int32, (obs, k_rows), 1).astype(jnp.float32)
    for i in range(own):
        a = act_s[me * own + i]
        row = bi[pl.ds(a, 1), i, :].astype(jnp.float32)
        col = jnp.sum(jnp.where(eye_o, row, 0.0), axis=1, keepdims=True)
        onehot[i * obs : (i + 1) * obs, :] = jnp.where(lanes == col, 1.0, 0.0).astype(jnp.bfloat16)

    mine_rows = pl.ds(pl.multiple_of(me * own, own), own)

    unit = mixf.shape[1]

    def mixture(c):
        def one_unit(u, carry):
            cols = pl.ds(pl.multiple_of(c * kw + u * unit, unit), unit)
            picked = jnp.dot(
                onehot[...], alphas_v[:, cols], preferred_element_type=jnp.float32
            )
            for i in range(own):
                a = act_s[me * own + i]
                weights = obs_v[a, :, cols].astype(jnp.float32)
                part = picked[i * obs : (i + 1) * obs, :] * weights
                mixf[i : i + 1, :] = jnp.sum(part, axis=0, keepdims=True)
            mix[mine_rows, cols] = mixf[...].astype(jnp.bfloat16)
            return carry

        lax.fori_loop(0, kw // unit, one_unit, 0)

    def send(c, src, dst, sem):
        piece = mix.at[pl.ds(pl.multiple_of(src * own, own), own), cols_of(c)]
        return pltpu.make_async_remote_copy(
            src_ref=piece,
            dst_ref=piece,
            send_sem=ag_send.at[c],
            recv_sem=sem.at[c],
            device_id={"bel": dst},
            device_id_type=MESH,
        )

    def some(c, count, sem):
        piece = mix.at[pl.ds(0, count * own), cols_of(c)]
        return pltpu.make_async_copy(piece, piece, sem.at[c])

    def each_peer(fn):
        def step(i, carry):
            fn(n_bel - 1 - i)
            return carry

        lax.fori_loop(0, n_bel - 1, step, 0, unroll=n_bel <= 8)

    ahead = min(AHEAD, n_ph)

    n_far = n_bel // 2
    far, near = me // 2, lax.rem(me, 2)
    other = far * 2 + 1 - near

    def far_peer(d):
        return lax.rem(far + d + n_far, n_far) * 2 + near

    def each_far(fn):
        def step(i, carry):
            fn(1 + i)
            return carry

        lax.fori_loop(0, n_far - 1, step, 0, unroll=n_far <= 4)

    def push(c):
        if c < DIRECT:
            each_peer(lambda d: send(c, me, lax.rem(me + d, n_bel), ag_recv).start())
        else:
            each_far(lambda d: send(c, me, far_peer(d), ag_far).start())
            send(c, me, other, ag_recv).start()

    def relay(c):
        some(c, n_far - 1, ag_far).wait()
        each_far(lambda d: send(c, far_peer(-d), other, ag_recv).start())

    def one_chunk(c, carry):
        load_alphas(c).wait()

        @pl.when(c == 0)
        def _():
            for later in range(1, n_ph):
                load_alphas(later).start()
            load_obs.wait()

        mixture(c)

        @pl.when(c == ahead - 1)
        def _():
            issue_w(0, False)
            pl.semaphore_wait(barrier, n_bel - 1 + n_st - 1)
            push(0)

        return carry

    lax.fori_loop(0, n_ph, one_chunk, 0)
    issue_w(0, True)
    if n_ph > 1:
        push(1)
        push(2)
        issue_w(1)
        relay(1)

    def arrive(c):
        some(c, n_bel - 1 if c < DIRECT else n_far, ag_recv).wait()

    def rs_copy(lo, size, k, d):
        peer = lax.rem(st + d, n_st)
        cols = pl.ds(pl.multiple_of(lo, tail), size)
        return pltpu.make_async_remote_copy(
            src_ref=terms.at[pl.ds(pl.multiple_of(peer * out_rows, out_rows), out_rows), cols],
            dst_ref=recv.at[d - 1, :, cols],
            send_sem=rs_send.at[k],
            recv_sem=rs_recv.at[k],
            device_id={"st": peer},
            device_id_type=MESH,
        )

    def product(a, rows, cols, r):
        part = slice(r * block, (r + 1) * block)
        keep = jnp.where(act_col[part, :] == float(a), 1.0, 0.0).astype(jnp.bfloat16)
        return lax.dot_general(
            w_v[a, rows, cols],
            mix[part, cols] * keep,
            (((1,), (1,)), ((), ())),
            preferred_element_type=jnp.float32,
        )

    def products(rows, cols, r):
        total = product(0, rows, cols, r)
        for a in range(1, acts):
            total += product(a, rows, cols, r)
        return total

    def finish(lo, size, k, cols, add):
        rows = pl.ds(pl.multiple_of(lo, tail), size)
        for r in range(beliefs // block):
            total = products(rows, cols, r)
            if add:
                total += acc[r, rows, :]
            terms[r * block : (r + 1) * block, rows] = total.T
        for d in range(1, n_st):
            rs_copy(lo, size, k, d).start()

    if n_ph > 1:
        steps = head * nj + early

        def partial(i, carry):
            p, j = i // nj, lax.rem(i, nj)

            for c in range(head + 1):

                @pl.when(i == c * nj)
                def _(c=c):
                    arrive(c)

            for c in range(3, n_ph):

                @pl.when(i == min(PUSHES[c], steps - 1))
                def _(c=c):
                    push(c)

            for c in range(2, n_ph):

                @pl.when(i == min(RELAYS[c], steps - 1))
                def _(c=c):
                    relay(c)

            await_w(p, j)
            rows = pl.ds(pl.multiple_of(j * nb, nb), nb)
            for r in range(beliefs // block):
                total = products(rows, cols_of(p), r)
                acc[r, rows, :] = jnp.where(p == 0, total, acc[r, rows, :] + total)
            for q in range(2, n_ph):

                @pl.when(i == (q - 2) * nj)
                def _():
                    issue_w(q)

            return carry

        lax.fori_loop(0, steps, partial, 0)
        if early == 0:
            arrive(n_ph - 2)
        arrive(n_ph - 1)

        def whole_block(j, carry):
            await_w(n_ph - 1, j)
            finish(j * nb, nb, j, cols_of(n_ph - 1), True)
            return carry

        lax.fori_loop(0, early, whole_block, 0)
        await_w(n_ph - 2, nj - 1)
        await_w(n_ph - 1, nj - 1)
    else:
        arrive(0)
        for j in range(nj):
            await_w(0, j)

    def tail_block(t, carry):
        left = slice(head * kw, depth)
        finish(early * nb + t * tail, tail, early + t, left, head > 0)
        return carry

    lax.fori_loop(0, (states - early * nb) // tail, tail_block, 0)

    mine = pl.ds(pl.multiple_of(st * out_rows, out_rows), out_rows)
    which = act_col[mine, :]

    for c in range(n_ph):
        some(c, n_bel - 1, ag_send).wait()

    def pieces(k, sem):
        lo, size = blocks[k]
        part = recv.at[:, :, pl.ds(lo, size)]
        return pltpu.make_async_copy(part, part, sem.at[k])

    def write_out(k):
        lo, size = blocks[k]
        return pltpu.make_async_copy(
            out_v.at[:, pl.ds(lo, size)], out_h.at[:, pl.ds(lo, size)], out_sem.at[k]
        )

    for k, (lo, size) in enumerate(blocks):
        cols = slice(lo, lo + size)
        gained = jnp.zeros((out_rows, size), jnp.float32)
        for a in range(acts):
            gained += jnp.where(
                which == float(a), reward[a : a + 1, cols].astype(jnp.float32), 0.0
            )
        total = terms[mine, cols]
        pieces(k, rs_recv).wait()
        for d in range(1, n_st):
            total += recv[d - 1, :, cols]
        out_v[:, cols] = (gained + scale * total).astype(out_v.dtype)
        write_out(k).start()

    for k in range(len(blocks)):
        pieces(k, rs_send).wait()
    for k in range(len(blocks)):
        write_out(k).wait()


def body(n_bel, n_st, alphas, transitions, observe, reward, belief_index, action):
    k_rows, depth = alphas.shape
    acts, states, _ = transitions.shape
    obs = observe.shape[1]
    own = belief_index.shape[0]
    beliefs = action.shape[0]
    out_rows = beliefs // n_st
    block = math.gcd(beliefs, 128)
    nb = math.gcd(states, 768) if states % 128 == 0 else states
    tail = math.gcd(nb, 256) if nb % 128 == 0 else nb
    nj = states // nb
    n_ph = PHASES if depth % (PHASES * 128) == 0 else 1
    kw = depth // n_ph
    unit = UNIT if kw % UNIT == 0 else kw
    n_blocks = (nj - 1 + nb // tail) if n_ph > 1 else states // tail
    scale = discount / (depth * n_st)
    hbm = pl.BlockSpec(memory_space=pl.ANY)
    return pl.pallas_call(
        functools.partial(kernel, n_bel, n_st, scale, n_ph, nb, tail),
        out_shape=jax.ShapeDtypeStruct((out_rows, states), jnp.bfloat16),
        in_specs=[hbm] * 7,
        out_specs=hbm,
        scratch_shapes=[
            pltpu.SMEM((beliefs,), jnp.int32),
            pltpu.VMEM((beliefs // block, block), jnp.int32),
            pltpu.VMEM((acts, own, obs), jnp.int32),
            pltpu.VMEM((acts, states), jnp.bfloat16),
            pltpu.VMEM((16, 128) if states >= k_rows else (k_rows, depth), jnp.bfloat16),
            pltpu.VMEM((acts, obs, depth), jnp.bfloat16),
            pltpu.VMEM((acts, states, depth), jnp.bfloat16),
            pltpu.VMEM((own * obs, k_rows), jnp.bfloat16),
            pltpu.VMEM((beliefs, 1), jnp.float32),
            pltpu.VMEM((own, unit), jnp.float32),
            pltpu.VMEM((beliefs, depth), jnp.bfloat16),
            pltpu.VMEM((beliefs // block, states, block), jnp.float32),
            pltpu.VMEM((beliefs, states), jnp.float32),
            pltpu.VMEM((n_st - 1, out_rows, states), jnp.float32),
            pltpu.VMEM((out_rows, states), jnp.bfloat16),
            pltpu.SemaphoreType.DMA((4,)),
            pltpu.SemaphoreType.DMA((n_ph + 1,)),
            pltpu.SemaphoreType.DMA((n_ph, nj, acts)),
            pltpu.SemaphoreType.DMA((n_blocks,)),
            pltpu.SemaphoreType.DMA((n_ph,)),
            pltpu.SemaphoreType.DMA((n_ph,)),
            pltpu.SemaphoreType.DMA((n_ph,)),
            pltpu.SemaphoreType.DMA((n_blocks,)),
            pltpu.SemaphoreType.DMA((n_blocks,)),
        ],
        compiler_params=pltpu.CompilerParams(
            collective_id=0, has_side_effects=True, vmem_limit_bytes=VMEM_BYTES
        ),
    )(
        action,
        action.reshape(beliefs // block, block),
        belief_index.transpose(1, 0, 2),
        reward,
        alphas,
        observe,
        transitions,
    )


def solution(mesh):
    placed = (
        P(None, "st"),
        P(None, "bel", "st"),
        P(None, None, "st"),
        P(None, "bel"),
        P("bel", None, None),
        P(),
    )
    return jax.shard_map(
        functools.partial(body, mesh.shape["bel"], mesh.shape["st"]),
        mesh=mesh,
        in_specs=placed,
        out_specs=P("st", "bel"),
        check_vma=False,
    )
```

```python
import functools
import math

import jax
import jax.numpy as jnp
from jax import lax
from jax.experimental import pallas as pl
from jax.experimental.pallas import tpu as pltpu
from jax.sharding import PartitionSpec as P

discount = 0.95
MESH = pl.DeviceIdType.MESH
VMEM_BYTES = 67_043_328
UNIT = 256
PHASES = 4
AHEAD = 1
PUSHES = (0, 0, 0, 0)
RELAYS = (0, 0, 1, 2)
DIRECT = 1


def kernel(
    n_bel,
    n_st,
    scale,
    n_ph,
    nb,
    tail,
    act_h,
    act_row_h,
    bi_h,
    reward_h,
    alphas_h,
    obs_h,
    w_h,
    out_h,
    act_s,
    act_row,
    bi,
    reward,
    spare,
    obs_v,
    w_v,
    onehot,
    act_col,
    mixf,
    mix,
    acc,
    terms,
    recv,
    out_v,
    in_sem,
    ao_sem,
    w_sem,
    out_sem,
    ag_send,
    ag_recv,
    ag_far,
    rs_send,
    rs_recv,
):
    acts, own, obs = bi.shape
    k_rows = alphas_h.shape[0]
    beliefs, depth = mix.shape
    states = w_v.shape[1]
    out_rows = out_v.shape[0]
    block = act_row.shape[1]
    kw = depth // n_ph
    nj = states // nb
    fits = states >= k_rows
    alphas_v = w_v.at[acts - 1, states - k_rows :, :] if fits else spare
    early = nj - 1 if n_ph > 1 else 0
    head = max(n_ph - 2, 0)
    blocks = [(j * nb, nb) for j in range(early)]
    blocks += [(lo, tail) for lo in range(early * nb, states, tail)]

    me = lax.axis_index("bel")
    st = lax.axis_index("st")

    barrier = pltpu.get_barrier_semaphore()
    for d in range(1, n_bel):
        pl.semaphore_signal(
            barrier, inc=1, device_id={"bel": lax.rem(me + d, n_bel)}, device_id_type=MESH
        )
    for d in range(1, n_st):
        pl.semaphore_signal(
            barrier, inc=1, device_id={"st": lax.rem(st + d, n_st)}, device_id_type=MESH
        )

    small = [
        pltpu.make_async_copy(src, dst, in_sem.at[i])
        for i, (src, dst) in enumerate(
            ((act_h, act_s), (bi_h, bi), (act_row_h, act_row), (reward_h, reward))
        )
    ]

    def cols_of(c):
        if n_ph == 1:
            return pl.ds(0, depth)
        return pl.ds(pl.multiple_of(c * kw, kw), kw)

    def load_alphas(c):
        return pltpu.make_async_copy(
            alphas_h.at[:, cols_of(c)], alphas_v.at[:, cols_of(c)], ao_sem.at[c]
        )

    load_obs = pltpu.make_async_copy(obs_h, obs_v, ao_sem.at[n_ph])

    def load_w(p, j, a):
        rows = pl.ds(pl.multiple_of(j * nb, nb), nb)
        return pltpu.make_async_copy(
            w_h.at[a, rows, cols_of(p)], w_v.at[a, rows, cols_of(p)], w_sem.at[p, j, a]
        )

    def shared(j, a):
        return fits and a == acts - 1 and (j + 1) * nb > states - k_rows

    def issue_w(p, late=None):
        for j in range(nj):
            for a in range(acts):
                if late is None or shared(j, a) == late:
                    load_w(p, j, a).start()

    def await_w(p, j):
        for a in range(acts):
            load_w(p, j, a).wait()

    for copy in small:
        copy.start()
    load_alphas(0).start()
    load_obs.start()

    for copy in small:
        copy.wait()

    eye = lax.broadcasted_iota(jnp.int32, (block, block), 0) == lax.broadcasted_iota(
        jnp.int32, (block, block), 1
    )
    for r in range(beliefs // block):
        row = act_row[r : r + 1, :].astype(jnp.float32)
        act_col[r * block : (r + 1) * block, :] = jnp.sum(
            jnp.where(eye, row, 0.0), axis=1, keepdims=True
        )
    eye_o = lax.broadcasted_iota(jnp.int32, (obs, obs), 0) == lax.broadcasted_iota(
        jnp.int32, (obs, obs), 1
    )
    lanes = lax.broadcasted_iota(jnp.int32, (obs, k_rows), 1).astype(jnp.float32)
    for i in range(own):
        a = act_s[me * own + i]
        row = bi[pl.ds(a, 1), i, :].astype(jnp.float32)
        col = jnp.sum(jnp.where(eye_o, row, 0.0), axis=1, keepdims=True)
        onehot[i * obs : (i + 1) * obs, :] = jnp.where(lanes == col, 1.0, 0.0).astype(jnp.bfloat16)

    mine_rows = pl.ds(pl.multiple_of(me * own, own), own)

    unit = mixf.shape[1]

    def mixture(c):
        def one_unit(u, carry):
            cols = pl.ds(pl.multiple_of(c * kw + u * unit, unit), unit)
            picked = jnp.dot(
                onehot[...], alphas_v[:, cols], preferred_element_type=jnp.float32
            )
            for i in range(own):
                a = act_s[me * own + i]
                weights = obs_v[a, :, cols].astype(jnp.float32)
                part = picked[i * obs : (i + 1) * obs, :] * weights
                mixf[i : i + 1, :] = jnp.sum(part, axis=0, keepdims=True)
            mix[mine_rows, cols] = mixf[...].astype(jnp.bfloat16)
            return carry

        lax.fori_loop(0, kw // unit, one_unit, 0)

    def send(c, src, dst, sem):
        piece = mix.at[pl.ds(pl.multiple_of(src * own, own), own), cols_of(c)]
        return pltpu.make_async_remote_copy(
            src_ref=piece,
            dst_ref=piece,
            send_sem=ag_send.at[c],
            recv_sem=sem.at[c],
            device_id={"bel": dst},
            device_id_type=MESH,
        )

    def some(c, count, sem):
        piece = mix.at[pl.ds(0, count * own), cols_of(c)]
        return pltpu.make_async_copy(piece, piece, sem.at[c])

    def each_peer(fn):
        def step(i, carry):
            fn(1 + lax.rem(i + n_bel // 2 - 1, n_bel - 1))
            return carry

        lax.fori_loop(0, n_bel - 1, step, 0, unroll=n_bel <= 8)

    ahead = min(AHEAD, n_ph)

    n_far = n_bel // 2
    far, near = me // 2, lax.rem(me, 2)
    other = far * 2 + 1 - near

    def far_peer(d):
        return lax.rem(far + d + n_far, n_far) * 2 + near

    def each_far(fn):
        def step(i, carry):
            fn(1 + i)
            return carry

        lax.fori_loop(0, n_far - 1, step, 0, unroll=n_far <= 4)

    def push(c):
        if c < DIRECT:
            each_peer(lambda d: send(c, me, lax.rem(me + d, n_bel), ag_recv).start())
        else:
            each_far(lambda d: send(c, me, far_peer(d), ag_far).start())
            send(c, me, other, ag_recv).start()

    def relay(c):
        some(c, n_far - 1, ag_far).wait()
        each_far(lambda d: send(c, far_peer(-d), other, ag_recv).start())

    def one_chunk(c, carry):
        load_alphas(c).wait()

        @pl.when(c == 0)
        def _():
            for later in range(1, n_ph):
                load_alphas(later).start()
            load_obs.wait()

        mixture(c)

        @pl.when(c == ahead - 1)
        def _():
            issue_w(0, False)
            pl.semaphore_wait(barrier, n_bel - 1 + n_st - 1)
            push(0)

        return carry

    lax.fori_loop(0, n_ph, one_chunk, 0)
    issue_w(0, True)
    if n_ph > 1:
        push(1)
        push(2)
        issue_w(1)
        relay(1)

    def arrive(c):
        some(c, n_bel - 1 if c < DIRECT else n_far, ag_recv).wait()

    def rs_copy(lo, size, k, d):
        peer = lax.rem(st + d, n_st)
        cols = pl.ds(pl.multiple_of(lo, tail), size)
        return pltpu.make_async_remote_copy(
            src_ref=terms.at[pl.ds(pl.multiple_of(peer * out_rows, out_rows), out_rows), cols],
            dst_ref=recv.at[d - 1, :, cols],
            send_sem=rs_send.at[k],
            recv_sem=rs_recv.at[k],
            device_id={"st": peer},
            device_id_type=MESH,
        )

    def product(a, rows, cols, r):
        part = slice(r * block, (r + 1) * block)
        keep = jnp.where(act_col[part, :] == float(a), 1.0, 0.0).astype(jnp.bfloat16)
        return lax.dot_general(
            w_v[a, rows, cols],
            mix[part, cols] * keep,
            (((1,), (1,)), ((), ())),
            preferred_element_type=jnp.float32,
        )

    def products(rows, cols, r):
        total = product(0, rows, cols, r)
        for a in range(1, acts):
            total += product(a, rows, cols, r)
        return total

    def finish(lo, size, k, cols, add):
        rows = pl.ds(pl.multiple_of(lo, tail), size)
        for r in range(beliefs // block):
            total = products(rows, cols, r)
            if add:
                total += acc[r, rows, :]
            terms[r * block : (r + 1) * block, rows] = total.T
        for d in range(1, n_st):
            rs_copy(lo, size, k, d).start()

    if n_ph > 1:
        steps = head * nj + early

        def partial(i, carry):
            p, j = i // nj, lax.rem(i, nj)

            for c in range(head + 1):

                @pl.when(i == c * nj)
                def _(c=c):
                    arrive(c)

            for c in range(3, n_ph):

                @pl.when(i == min(PUSHES[c], steps - 1))
                def _(c=c):
                    push(c)

            for c in range(2, n_ph):

                @pl.when(i == min(RELAYS[c], steps - 1))
                def _(c=c):
                    relay(c)

            await_w(p, j)
            rows = pl.ds(pl.multiple_of(j * nb, nb), nb)
            for r in range(beliefs // block):
                total = products(rows, cols_of(p), r)
                acc[r, rows, :] = jnp.where(p == 0, total, acc[r, rows, :] + total)
            for q in range(2, n_ph):

                @pl.when(i == (q - 2) * nj)
                def _():
                    issue_w(q)

            return carry

        lax.fori_loop(0, steps, partial, 0)
        if early == 0:
            arrive(n_ph - 2)
        arrive(n_ph - 1)

        def whole_block(j, carry):
            await_w(n_ph - 1, j)
            finish(j * nb, nb, j, cols_of(n_ph - 1), True)
            return carry

        lax.fori_loop(0, early, whole_block, 0)
        await_w(n_ph - 2, nj - 1)
        await_w(n_ph - 1, nj - 1)
    else:
        arrive(0)
        for j in range(nj):
            await_w(0, j)

    def tail_block(t, carry):
        left = slice(head * kw, depth)
        finish(early * nb + t * tail, tail, early + t, left, head > 0)
        return carry

    lax.fori_loop(0, (states - early * nb) // tail, tail_block, 0)

    mine = pl.ds(pl.multiple_of(st * out_rows, out_rows), out_rows)
    which = act_col[mine, :]

    for c in range(n_ph):
        some(c, n_bel - 1, ag_send).wait()

    def pieces(k, sem):
        lo, size = blocks[k]
        part = recv.at[:, :, pl.ds(lo, size)]
        return pltpu.make_async_copy(part, part, sem.at[k])

    def write_out(k):
        lo, size = blocks[k]
        return pltpu.make_async_copy(
            out_v.at[:, pl.ds(lo, size)], out_h.at[:, pl.ds(lo, size)], out_sem.at[k]
        )

    for k, (lo, size) in enumerate(blocks):
        cols = slice(lo, lo + size)
        gained = jnp.zeros((out_rows, size), jnp.float32)
        for a in range(acts):
            gained += jnp.where(
                which == float(a), reward[a : a + 1, cols].astype(jnp.float32), 0.0
            )
        total = terms[mine, cols]
        pieces(k, rs_recv).wait()
        for d in range(1, n_st):
            total += recv[d - 1, :, cols]
        out_v[:, cols] = (gained + scale * total).astype(out_v.dtype)
        write_out(k).start()

    for k in range(len(blocks)):
        pieces(k, rs_send).wait()
    for k in range(len(blocks)):
        write_out(k).wait()


def body(n_bel, n_st, alphas, transitions, observe, reward, belief_index, action):
    k_rows, depth = alphas.shape
    acts, states, _ = transitions.shape
    obs = observe.shape[1]
    own = belief_index.shape[0]
    beliefs = action.shape[0]
    out_rows = beliefs // n_st
    block = math.gcd(beliefs, 128)
    nb = math.gcd(states, 768) if states % 128 == 0 else states
    tail = math.gcd(nb, 256) if nb % 128 == 0 else nb
    nj = states // nb
    n_ph = PHASES if depth % (PHASES * 128) == 0 else 1
    kw = depth // n_ph
    unit = UNIT if kw % UNIT == 0 else kw
    n_blocks = (nj - 1 + nb // tail) if n_ph > 1 else states // tail
    scale = discount / (depth * n_st)
    hbm = pl.BlockSpec(memory_space=pl.ANY)
    return pl.pallas_call(
        functools.partial(kernel, n_bel, n_st, scale, n_ph, nb, tail),
        out_shape=jax.ShapeDtypeStruct((out_rows, states), jnp.bfloat16),
        in_specs=[hbm] * 7,
        out_specs=hbm,
        scratch_shapes=[
            pltpu.SMEM((beliefs,), jnp.int32),
            pltpu.VMEM((beliefs // block, block), jnp.int32),
            pltpu.VMEM((acts, own, obs), jnp.int32),
            pltpu.VMEM((acts, states), jnp.bfloat16),
            pltpu.VMEM((16, 128) if states >= k_rows else (k_rows, depth), jnp.bfloat16),
            pltpu.VMEM((acts, obs, depth), jnp.bfloat16),
            pltpu.VMEM((acts, states, depth), jnp.bfloat16),
            pltpu.VMEM((own * obs, k_rows), jnp.bfloat16),
            pltpu.VMEM((beliefs, 1), jnp.float32),
            pltpu.VMEM((own, unit), jnp.float32),
            pltpu.VMEM((beliefs, depth), jnp.bfloat16),
            pltpu.VMEM((beliefs // block, states, block), jnp.float32),
            pltpu.VMEM((beliefs, states), jnp.float32),
            pltpu.VMEM((n_st - 1, out_rows, states), jnp.float32),
            pltpu.VMEM((out_rows, states), jnp.bfloat16),
            pltpu.SemaphoreType.DMA((4,)),
            pltpu.SemaphoreType.DMA((n_ph + 1,)),
            pltpu.SemaphoreType.DMA((n_ph, nj, acts)),
            pltpu.SemaphoreType.DMA((n_blocks,)),
            pltpu.SemaphoreType.DMA((n_ph,)),
            pltpu.SemaphoreType.DMA((n_ph,)),
            pltpu.SemaphoreType.DMA((n_ph,)),
            pltpu.SemaphoreType.DMA((n_blocks,)),
            pltpu.SemaphoreType.DMA((n_blocks,)),
        ],
        compiler_params=pltpu.CompilerParams(
            collective_id=0, has_side_effects=True, vmem_limit_bytes=VMEM_BYTES
        ),
    )(
        action,
        action.reshape(beliefs // block, block),
        belief_index.transpose(1, 0, 2),
        reward,
        alphas,
        observe,
        transitions,
    )


def solution(mesh):
    placed = (
        P(None, "st"),
        P(None, "bel", "st"),
        P(None, None, "st"),
        P(None, "bel"),
        P("bel", None, None),
        P(),
    )
    return jax.shard_map(
        functools.partial(body, mesh.shape["bel"], mesh.shape["st"]),
        mesh=mesh,
        in_specs=placed,
        out_specs=P("st", "bel"),
        check_vma=False,
    )
```
